32 devices in a mesh: dp: 4 (over z), mp: 8 (over y, x, core).
Axes of the slice: x: 2, y: 2, z: 4, core: 2. Of those that a mesh axis runs over, the one named last changes fastest.
Arguments:
- gate_pre: bfloat16 [768, 14336], P('dp', 'mp'), may hold values from -8 to 8
- up_pre: bfloat16 [768, 14336], P('dp', 'mp'), may hold values from -6 to 6
- d_out: bfloat16 [768, 4096], P(('dp', 'mp')), may hold values from -6 to 6
- down_weight: bfloat16 [4096, 14336], P('dp', 'mp'), may hold values from -0.046875 to 0.046875
Outputs:
- d_gate: bfloat16 [768, 14336], P('dp', 'mp')
- d_up: bfloat16 [768, 14336], P('dp', 'mp')
- grad_down: bfloat16 [4096, 14336], P('dp', 'mp')
The draws below stay inside these ranges and needn't reach their ends.
All inputs are finite; a program needn't handle non-finite values.
Results may differ from the reference program's by a relative error of at most 0.0095.
Values may be sent and summed in bfloat16 or wider, within the bound.
A program may use at most 128 MiB of HBM per device.

```python
import jax
import jax.numpy as jnp
from jax import lax

D = 4096
FF = 14336
TOK_DEV = 24
TOKENS = 768
N_DP = 4
N_MP = 8


def raised(array, stream_key, source, target, parts, factor):
    owner, partner = [(jnp.arange(array.shape[position]) // (array.shape[position] // parts)).reshape([-1 if axis == position else 1 for axis in range(array.ndim)]) for position in (source, target)]
    chosen = jax.random.permutation(stream_key, parts)[partner]
    strong = (owner == chosen) | (owner == (partner + parts // 2) % parts)
    return jnp.where(strong, factor * array, array)


def steps_of(rng, dims, shards, smallest, high):
    level, own = 1.0, jax.random.fold_in(rng, 6)
    for axis_at, shards_of in shards:
        heights = jnp.exp(jax.random.uniform(jax.random.fold_in(own, axis_at), (shards_of,), jnp.float32, smallest / len(shards), high / len(shards)))
        level = level * jnp.repeat(heights, dims[axis_at] // shards_of).reshape([-1 if axis == axis_at else 1 for axis in range(len(dims))])
    return level


def centred(stream_key, shape, scale, bound, pieces=(), held_as=jnp.bfloat16):
    entries = jax.random.normal(stream_key, shape, jnp.float32) * scale
    if len(pieces) > 0:
        entries = steps_of(stream_key, shape, pieces, -0.22, 0.18) * entries
    return jnp.clip(entries, min=-bound, max=bound).astype(held_as)


def heavy_noise(stream_key, shape, width, limit, shards, heavy, kind=jnp.bfloat16):
    entries = width * jax.random.normal(stream_key, shape, jnp.float32)
    if shards:
        entries = entries * steps_of(stream_key, shape, shards, -0.22, 0.18)
    return jnp.clip(raised(entries, jax.random.fold_in(stream_key, 3), *heavy), -limit, limit).astype(kind)


def setup_inputs(seed: int = 0) -> dict:
    key_list = jax.random.split(jax.random.key(seed), 5)
    return {
        "gate_pre": centred(key_list[0], (TOKENS, FF), 2.0, 8.0, ((0, 4), (1, 8))),
        "up_pre": centred(key_list[1], (TOKENS, FF), 1.0, 6.0, ((0, 4), (1, 8))),
        "d_out": heavy_noise(key_list[2], (TOKENS, D), 1.0, 6.0, ((0, 32),), (0, 1, 32, 2.75)),
        "down_weight": centred(key_list[3], (D, FF), FF ** -0.5, 0.046875, ((0, 4), (1, 8))),
    }


def reference(gate_pre, up_pre, d_out, down_weight):
    gate = gate_pre.astype(jnp.float32)
    upper = up_pre.astype(jnp.float32)
    sig = jax.nn.sigmoid(gate)
    act = gate * sig
    hidden = (act * upper).astype(jnp.bfloat16)
    d_hidden = jnp.dot(d_out, down_weight, preferred_element_type=jnp.float32)
    d_up = (d_hidden * act).astype(jnp.bfloat16)
    d_gate = (d_hidden * upper * sig * (1.0 + gate * (1.0 - sig))).astype(jnp.bfloat16)
    tok_rows = TOK_DEV * N_MP

    def add_replica(total, index):
        start = (index * tok_rows).astype(jnp.int32)
        rows_out = lax.dynamic_slice_in_dim(d_out, start, tok_rows, 0)
        rows_hidden = lax.dynamic_slice_in_dim(hidden, start, tok_rows, 0)
        part = lax.dot_general(rows_out, rows_hidden, (((0,), (0,)), ((), ())), preferred_element_type=jnp.float32)
        return total + part.astype(jnp.bfloat16).astype(jnp.float32), None

    total, unused = lax.scan(add_replica, jnp.zeros((D, FF), jnp.float32), jnp.arange(N_DP, dtype=jnp.int32))
    grad_down = (total / N_DP).astype(jnp.bfloat16)
    return d_gate, d_up, grad_down
```

```python
import functools

import jax
import jax.numpy as jnp
from jax import lax
from jax.experimental import pallas as pl
from jax.experimental.pallas import tpu as pltpu
from jax.sharding import PartitionSpec as P

MESH = pl.DeviceIdType.MESH


def plain(gate_pre, up_pre, d_out, down_weight):
    replicas, peers = lax.axis_size("dp"), lax.axis_size("mp")
    rows, features = d_out.shape[0], down_weight.shape[0]
    gate = gate_pre.astype(jnp.float32)
    upper = up_pre.astype(jnp.float32)
    sig = jax.nn.sigmoid(gate)
    act = gate * sig
    hidden = (act * upper).astype(jnp.bfloat16)
    columns = lax.all_to_all(d_out, "dp", split_axis=1, concat_axis=0, tiled=True)
    columns = lax.all_gather(columns.reshape(replicas, rows, features), "mp", axis=1)
    columns = columns.reshape(replicas * peers * rows, features)
    every_hidden = lax.all_gather(hidden, "dp", axis=0, tiled=True)
    share = jnp.dot(columns, down_weight, preferred_element_type=jnp.float32)
    d_hidden = lax.psum_scatter(share, "dp", scatter_dimension=0, tiled=True)
    d_up = (d_hidden * act).astype(jnp.bfloat16)
    d_gate = (d_hidden * upper * sig * (1.0 + gate * (1.0 - sig))).astype(jnp.bfloat16)
    total = lax.dot_general(
        columns, every_hidden, (((0,), (0,)), ((), ())), preferred_element_type=jnp.float32
    )
    return d_gate, d_up, (total / replicas).astype(jnp.bfloat16)


def solution(mesh):
    in_specs = (P("dp", "mp"), P("dp", "mp"), P(("dp", "mp"), None), P("dp", "mp"))
    out_specs = (P("dp", "mp"), P("dp", "mp"), P("dp", "mp"))
    return jax.shard_map(plain, mesh=mesh, in_specs=in_specs, out_specs=out_specs, check_vma=False)
```
